32 devices in a mesh: lon: 16 (over z, x, core), obs: 2 (over y).
Axes of the slice: x: 2, y: 2, z: 4, core: 2. Of those that a mesh axis runs over, the one named last changes fastest.
Arguments:
- perturb: float32 [16384, 1024], P('lon'), may hold values from -6 to 6
- observed: bfloat16 [4096, 1024], P(('lon', 'obs')), may hold values from -6 to 6
- solved: bfloat16 [4096, 1024], P(('lon', 'obs')), may hold values from -6 to 6
- taper_index: int32 [16384, 1792], P('lon', 'obs'), may hold values from 0 to 15
- taper_table: float32 [16], replicated, may hold values from 0.05 to 1
Outputs:
- analysis: float32 [16384, 1024], P(('lon', 'obs'))
The draws below stay inside these ranges and needn't reach their ends.
All inputs are finite; a program needn't handle non-finite values.
Results may differ from the reference program's by a relative error of at most 0.0035.
Values may be sent and summed in bfloat16 or wider, within the bound.
No kernel may reach another device: no remote copies, remote signals or barrier semaphores. Data moves between devices by JAX's collectives and lax.ppermute only.
A program may use at most 128 MiB of HBM per device.

```python
import math
import jax
import jax.numpy as jnp
from jax import lax

MEMBERS = 1024
PTS_TILE = 1024
OBS_DEV = 128
REACH = 3
LEVELS = 16
NPTS = 16384
NOBS = 4096
WINDOW = 1792
N_LON = 16
N_OBS = 2


def touch_ends(entries, stream_key, low, high):
    longest = entries.shape.index(max(entries.shape))
    spots = []
    for shift in (0, 1):
        where = [jax.random.randint(jax.random.fold_in(stream_key, axis), (), 0, length) for axis, length in enumerate(entries.shape)]
        where[longest] = (where[longest] + shift) % entries.shape[longest]
        spots.append(tuple(where))
    return entries.at[spots[0]].set(low).at[spots[1]].set(high)


def levels(stream_key, extent, cuts, least, largest):
    gain, own = 1.0, jax.random.fold_in(stream_key, 6)
    for axis_at, shards_of in cuts:
        draws = jnp.exp(jax.random.uniform(jax.random.fold_in(own, axis_at), (shards_of,), jnp.float32, least / len(cuts), largest / len(cuts)))
        gain = gain * jnp.repeat(draws, extent[axis_at] // shards_of).reshape([-1 if axis == axis_at else 1 for axis in range(len(extent))])
    return gain


def centred(rng, dims, spread, most, cuts=(), kind=jnp.bfloat16):
    array = spread * jax.random.normal(rng, dims, jnp.float32)
    if cuts:
        array = array * levels(rng, dims, cuts, -0.22, 0.18)
    return jnp.clip(array, -most, most).astype(kind)


def setup_inputs(seed: int = 0) -> dict:
    arg_keys = jax.random.split(jax.random.key(seed), 6)
    perturb = centred(arg_keys[0], (NPTS, MEMBERS), 1.0, 6.0, ((0, 16),), jnp.float32)
    observed = centred(arg_keys[1], (NOBS, MEMBERS), 1.0, 6.0, ((0, 32),))
    solved = centred(arg_keys[2], (NOBS, MEMBERS), 1.0, 6.0, ((0, 32),))
    taper_index = touch_ends(jax.random.randint(arg_keys[3], (NPTS, WINDOW), 0, LEVELS), jax.random.fold_in(arg_keys[3], 1), 0, LEVELS - 1).astype(jnp.int32)
    taper_table = jnp.clip(jnp.exp(jax.random.uniform(arg_keys[4], (LEVELS,), jnp.float32, math.log(0.05), math.log(1.0))), 0.05, 1.0)
    return dict(perturb=perturb, observed=observed, solved=solved, taper_index=taper_index, taper_table=taper_table)


def reference(perturb, observed, solved, taper_index, taper_table):
    span = 2 * REACH + 1
    obs_four = observed.reshape(N_LON, N_OBS, OBS_DEV, MEMBERS)
    sol_four = solved.reshape(N_LON, N_OBS, OBS_DEV, MEMBERS)
    tiles_x = perturb.reshape(N_LON, PTS_TILE, MEMBERS)
    tiles_i = taper_index.reshape(N_LON, PTS_TILE, N_OBS * span * OBS_DEV)

    def one_tile(packed):
        tile, xs, index_tile = packed
        near = (tile + jnp.arange(span, dtype=jnp.int32) - REACH) % N_LON
        y_win = jnp.transpose(obs_four[near], (1, 0, 2, 3)).reshape(-1, MEMBERS).astype(jnp.float32)
        z_win = jnp.transpose(sol_four[near], (1, 0, 2, 3)).reshape(-1, MEMBERS).astype(jnp.float32)
        x_half = xs.astype(jnp.bfloat16)
        x_half = lax.optimization_barrier(x_half).astype(jnp.float32)
        cov = jnp.dot(x_half, y_win.T, precision=lax.Precision.HIGHEST) / (MEMBERS - 1)
        rho = taper_table[index_tile]
        weighted = (rho * cov).astype(jnp.bfloat16)
        weighted = lax.optimization_barrier(weighted).astype(jnp.float32)
        return xs + jnp.dot(weighted, z_win, precision=lax.Precision.HIGHEST)

    result = lax.map(one_tile, (jnp.arange(N_LON, dtype=jnp.int32), tiles_x, tiles_i))
    return result.reshape(N_LON * PTS_TILE, MEMBERS)
```

```python
import functools

import jax
import jax.numpy as jnp
from jax import lax
from jax.experimental import pallas as pl
from jax.experimental.pallas import tpu as pltpu
from jax.sharding import PartitionSpec as P

REACH = 3
SPAN = 2 * REACH + 1


def permute(value, axis, target):
    count = lax.axis_size(axis)
    return lax.ppermute(value, axis, [(s, target(s) % count) for s in range(count)])


def swap(value):
    return permute(value, "lon", lambda s: s ^ 1)


def gather_window(block):
    up = permute(block, "lon", lambda s: s + 2)
    down = permute(block, "lon", lambda s: s - 2)
    far = permute(block, "lon", lambda s: s + 3 if s % 2 else s - 3)
    return (block, swap(block), up, swap(up), down, swap(down), far)


def slots():
    even = jnp.array([3, 4, 1, 2, 5, 6, 0], jnp.int32)
    odd = jnp.array([3, 2, 1, 0, 5, 4, 6], jnp.int32)
    return jnp.where(lax.axis_index("lon") % 2 == 0, even, odd)


def window_kernel(members, with_base, first, slot, table, x_ref, index_ref, *refs):
    ys, zs = refs[:SPAN], refs[SPAN : 2 * SPAN]
    out_ref, y_cat, z_cat, sems = refs[2 * SPAN :]
    width = ys[0].shape[0]

    def copies():
        for n in range(SPAN):
            rows = pl.ds(pl.multiple_of(slot[n] * width, width), width)
            yield pltpu.make_async_copy(ys[n], y_cat.at[rows], sems.at[0, n])
            yield pltpu.make_async_copy(zs[n], z_cat.at[rows], sems.at[1, n])

    @pl.when(pl.program_id(0) == 0)
    def _():
        for c in copies():
            c.start()
        for c in copies():
            c.wait()

    lanes = lax.broadcasted_iota(jnp.int32, (8, 128), 1)
    levels = jnp.zeros((8, 128), jnp.float32)
    for level in range(table.shape[0]):
        levels = jnp.where(lanes == level, table[level], levels)
    levels = levels / (members - 1)

    x = x_ref[...]
    tile = x.shape[0]
    cov = lax.dot_general(
        x.astype(jnp.bfloat16),
        y_cat[...],
        (((1,), (1,)), ((), ())),
        preferred_element_type=jnp.float32,
    )
    spread = jnp.broadcast_to(levels[:1], (tile, 128))
    weighted = []
    for c in range(index_ref.shape[1] // 128):
        cols = slice(c * 128, (c + 1) * 128)
        rho = jnp.take_along_axis(spread, index_ref[:, cols], axis=1, mode="promise_in_bounds")
        weighted.append((rho * cov[:, cols]).astype(jnp.bfloat16))
    total = jnp.dot(
        jnp.concatenate(weighted, axis=1), z_cat[...], preferred_element_type=jnp.float32
    )
    if with_base:
        total = total + x
    out_ref[...] = total.astype(out_ref.dtype)


def window_term(perturb, taper_index, taper_table, ys, zs, slot, part, share, with_base):
    members = perturb.shape[1]
    width = ys[0].shape[0]
    tile = min(share, 256)
    steps = share // tile
    first = (part * steps).astype(jnp.int32).reshape(1)
    dtype = jnp.float32 if with_base else jnp.bfloat16
    row_map = lambda i, first, *_: (first[0] + i, 0)
    anywhere = pl.BlockSpec(memory_space=pl.ANY)
    columns = SPAN * width
    return pl.pallas_call(
        functools.partial(window_kernel, members, with_base),
        out_shape=jax.ShapeDtypeStruct((share, members), dtype),
        grid_spec=pltpu.PrefetchScalarGridSpec(
            num_scalar_prefetch=3,
            grid=(steps,),
            in_specs=[
                pl.BlockSpec((tile, members), row_map),
                pl.BlockSpec((tile, columns), row_map),
            ]
            + [anywhere] * (2 * SPAN),
            out_specs=pl.BlockSpec((tile, members), lambda i, *_: (i, 0)),
            scratch_shapes=[
                pltpu.VMEM((columns, members), jnp.bfloat16),
                pltpu.VMEM((columns, members), jnp.bfloat16),
                pltpu.SemaphoreType.DMA((2, SPAN)),
            ],
        ),
        compiler_params=pltpu.CompilerParams(dimension_semantics=("arbitrary",)),
        cost_estimate=pl.CostEstimate(
            flops=4 * share * columns * members,
            bytes_accessed=share * (members * 8 + columns * 4) + 4 * columns * members,
            transcendentals=0,
        ),
        name="window_own" if with_base else "window_sent",
    )(first, slot, taper_table, perturb, taper_index, *ys, *zs)


def per_device(perturb, observed, solved, taper_index, taper_table):
    groups = lax.axis_size("obs")
    me = lax.axis_index("obs")
    share = perturb.shape[0] // groups
    ys = gather_window(observed)
    zs = gather_window(solved)
    slot = slots()
    term = functools.partial(window_term, perturb, taper_index, taper_table, ys, zs, slot)
    came = []
    for step in range(1, groups):
        piece = term((me + step) % groups, share, False)
        came.append(permute(piece, "obs", lambda s: s + step))
    total = term(me, share, True)
    for piece in came:
        total = total + piece.astype(jnp.float32)
    return total


def solution(mesh):
    placed = (
        P("lon", None),
        P(("lon", "obs"), None),
        P(("lon", "obs"), None),
        P("lon", "obs"),
        P(),
    )
    return jax.shard_map(
        per_device, mesh=mesh, in_specs=placed, out_specs=P(("lon", "obs"), None), check_vma=False
    )
```

```python
import functools
import math

import jax
import jax.numpy as jnp
from jax import lax
from jax.experimental import pallas as pl
from jax.experimental.pallas import tpu as pltpu
from jax.sharding import PartitionSpec as P


REACH = 3
SPAN = 2 * REACH + 1
LANES = 128
VMEM_LIMIT = 24 * 1024 * 1024


WHOLE = pl.BlockSpec(memory_space=pltpu.VMEM)
SCALARS = pl.BlockSpec(memory_space=pltpu.SMEM)
PARAMS = pltpu.CompilerParams(vmem_limit_bytes=VMEM_LIMIT)


def permute(value, axis, target):
    count = lax.axis_size(axis)
    return lax.ppermute(value, axis, [(s, target(s) % count) for s in range(count)])


def swap(value):
    return permute(value, "lon", lambda s: s ^ 1)


def gather_far(block):
    up = permute(block, "lon", lambda s: s + 2)
    down = permute(block, "lon", lambda s: s - 2)
    far = permute(block, "lon", lambda s: s + 3 if s % 2 else s - 3)
    return (up, swap(up), down, swap(down), far)


def slots():
    even = jnp.array([3, 4, 1, 2, 5, 6, 0], jnp.int32)
    odd = jnp.array([3, 2, 1, 0, 5, 4, 6], jnp.int32)
    return jnp.where(lax.axis_index("lon") % 2 == 0, even, odd)


def member_cut(members):
    return members - max(LANES, members * 3 // 8 // LANES * LANES)


def scaled_levels(table, members):
    lanes = lax.broadcasted_iota(jnp.int32, (8, LANES), 1)
    levels = jnp.zeros((8, LANES), jnp.float32)
    for level in range(table.shape[0]):
        levels = jnp.where(lanes == level, table[level], levels)
    return levels[:1] / (members - 1)


def tapered(levels, index, cov):
    spread = jnp.broadcast_to(levels, index.shape)
    rho = jnp.take_along_axis(spread, index, axis=1, mode="promise_in_bounds")
    return (rho * cov).astype(jnp.bfloat16)


def contract(x, y):
    return lax.dot_general(
        x, y, (((1,), (1,)), ((), ())), preferred_element_type=jnp.float32
    )


def pack_kernel(y_ref, z_ref, first_ref, rest_ref, sems):
    members, cut = z_ref.shape[1], rest_ref.shape[1]
    copies = [
        pltpu.make_async_copy(source, target, sems.at[n])
        for n, (source, target) in enumerate(
            (
                (y_ref, first_ref.at[:, :members]),
                (z_ref.at[:, cut:], first_ref.at[:, members:]),
                (z_ref.at[:, :cut], rest_ref),
            )
        )
    ]
    for copy in copies:
        copy.start()
    for copy in copies:
        copy.wait()


def pack(y, z, cut):
    width, members = z.shape
    return pl.pallas_call(
        pack_kernel,
        out_shape=[
            jax.ShapeDtypeStruct((width, 2 * members - cut), z.dtype),
            jax.ShapeDtypeStruct((width, cut), z.dtype),
        ],
        in_specs=[pl.BlockSpec(memory_space=pl.ANY)] * 2,
        out_specs=[WHOLE] * 2,
        scratch_shapes=[pltpu.SemaphoreType.DMA((3,))],
        compiler_params=PARAMS,
        name="pack",
    )(in_hbm(y), in_hbm(z))


def near_kernel(me, slot, table, x_ref, index_ref, y_own, y_near, xb_ref, w_ref, kept_ref):
    levels = scaled_levels(table, x_ref.shape[1])
    x = x_ref[...].astype(jnp.bfloat16)
    xb_ref[...] = x
    kept_ref[...] = index_ref[...].astype(jnp.int8)
    width = y_own.shape[0]
    for n, y in enumerate((y_own, y_near)):
        at = pl.ds(pl.multiple_of(slot[n] * width, width), width)
        w_ref[:, n * width : (n + 1) * width] = tapered(
            levels, index_ref[:, at], contract(x, y[:, : x.shape[1]])
        )


def near_terms(perturb, taper_index, table, me, slot, y_own, y_near, share):
    points, members = perturb.shape
    groups = points // share
    columns = taper_index.shape[1]
    width = y_own.shape[0]
    tile = min(share, 256)
    per = share // tile
    rows = points - share

    def source(i, me, *_):
        return (lax.rem(me[0] + 1 + i // per, groups) * per + i % per, 0)

    taken = lambda n: pl.BlockSpec((tile, n), source)
    row = lambda n: pl.BlockSpec((tile, n), lambda i, *_: (i, 0))
    full = pl.BlockSpec(y_own.shape, lambda i, *_: (0, 0))
    return pl.pallas_call(
        near_kernel,
        out_shape=[
            jax.ShapeDtypeStruct((rows, members), jnp.bfloat16),
            jax.ShapeDtypeStruct((rows, 2 * width), jnp.bfloat16),
            jax.ShapeDtypeStruct((rows, columns), jnp.int8),
        ],
        grid_spec=pltpu.PrefetchScalarGridSpec(
            num_scalar_prefetch=3,
            grid=(rows // tile,),
            in_specs=[taken(members), taken(columns), full, full],
            out_specs=[row(members), row(2 * width), row(columns)],
        ),
        compiler_params=PARAMS,
        cost_estimate=pl.CostEstimate(
            flops=4 * rows * width * members,
            bytes_accessed=rows * (members * 6 + columns * 5 + width * 4),
            transcendentals=0,
        ),
        name="near",
    )(me, slot, table, in_hbm(perturb), in_hbm(taper_index), y_own, y_near)


def in_hbm(value):
    return pltpu.with_memory_space_constraint(value, pltpu.MemorySpace.HBM)


def fill(cat, blocks, low, high):
    width = blocks[0].shape[0]
    for n, block in enumerate(blocks):
        cat[n * width : (n + 1) * width, :] = block[:, low:high]


def tapered_blocks(levels, slot, order, index_ref, cov, width):
    for n, position in enumerate(order):
        at = pl.ds(pl.multiple_of(slot[position] * width, width), width)
        index = index_ref[:, at].astype(jnp.int32)
        yield tapered(levels, index, cov[:, n * width : (n + 1) * width])


def weigh_kernel(slot, table, xb_ref, index_ref, near_ref, *refs):
    ys, (w_ref, y_cat) = refs[:-2], refs[-2:]
    levels = scaled_levels(table, xb_ref.shape[1])
    fill(y_cat, ys, 0, xb_ref.shape[1])
    width = ys[0].shape[0]
    tile = min(xb_ref.shape[0], 256)
    w_ref[:, : 2 * width] = near_ref[...]
    for at in range(0, xb_ref.shape[0], tile):
        rows = slice(at, at + tile)
        cov = contract(xb_ref[rows, :], y_cat[...])
        blocks = tapered_blocks(levels, slot, range(2, SPAN), index_ref.at[rows], cov, width)
        for n, block in enumerate(blocks, 2):
            w_ref[rows, n * width : (n + 1) * width] = block


def weigh(slot, table, xb, kept, near, ys):
    rows, members = xb.shape
    width = ys[0].shape[0]
    return pl.pallas_call(
        weigh_kernel,
        out_shape=jax.ShapeDtypeStruct((rows, SPAN * width), jnp.bfloat16),
        in_specs=[SCALARS] * 2 + [WHOLE] * (3 + len(ys)),
        out_specs=WHOLE,
        scratch_shapes=[pltpu.VMEM((len(ys) * width, members), jnp.bfloat16)],
        compiler_params=PARAMS,
        cost_estimate=pl.CostEstimate(
            flops=2 * rows * width * len(ys) * members,
            bytes_accessed=rows * width * 64,
            transcendentals=0,
        ),
        name="weigh",
    )(slot, table, xb, kept, near, *ys)


def weigh_own_kernel(me, slot, table, x_ref, index_ref, *refs):
    ys, (w_ref, y_cat) = refs[:-2], refs[-2:]
    width = ys[0].shape[0]

    @pl.when(pl.program_id(0) == 0)
    def _():
        fill(y_cat, ys, 0, x_ref.shape[1])

    levels = scaled_levels(table, x_ref.shape[1])
    cov = contract(x_ref[...].astype(jnp.bfloat16), y_cat[...])
    blocks = tapered_blocks(levels, slot, range(SPAN), index_ref, cov, width)
    for n, block in enumerate(blocks):
        w_ref[:, n * width : (n + 1) * width] = block


def weigh_own(me, slot, table, perturb, taper_index, ys, share):
    members, columns = perturb.shape[1], taper_index.shape[1]
    tile = min(share, 256)
    per = share // tile
    taken = lambda n: pl.BlockSpec((tile, n), lambda i, me, *_: (me[0] * per + i, 0))
    return pl.pallas_call(
        weigh_own_kernel,
        out_shape=jax.ShapeDtypeStruct((share, columns), jnp.bfloat16),
        grid_spec=pltpu.PrefetchScalarGridSpec(
            num_scalar_prefetch=3,
            grid=(per,),
            in_specs=[taken(members), taken(columns)] + [WHOLE] * len(ys),
            out_specs=pl.BlockSpec((tile, columns), lambda i, *_: (i, 0)),
            scratch_shapes=[pltpu.VMEM((columns, members), jnp.bfloat16)],
        ),
        compiler_params=PARAMS,
        cost_estimate=pl.CostEstimate(
            flops=2 * share * columns * members,
            bytes_accessed=share * (members * 4 + columns * 6),
            transcendentals=0,
        ),
        name="weigh_own",
    )(me, slot, table, in_hbm(perturb), in_hbm(taper_index), *ys)


def part_kernel(low, high, w_ref, *refs):
    zs, (p_ref, z_cat) = refs[:-2], refs[-2:]
    fill(z_cat, zs, low, high)
    tile = min(w_ref.shape[0], 256)
    for at in range(0, w_ref.shape[0], tile):
        p_ref[at : at + tile, :] = jnp.dot(
            w_ref[at : at + tile, :], z_cat[...], preferred_element_type=jnp.float32
        ).astype(p_ref.dtype)


def part_terms(w, zs, low, high):
    rows, columns = w.shape
    return pl.pallas_call(
        functools.partial(part_kernel, low, high),
        out_shape=jax.ShapeDtypeStruct((rows, high - low), jnp.bfloat16),
        in_specs=[WHOLE] * (1 + len(zs)),
        out_specs=WHOLE,
        scratch_shapes=[pltpu.VMEM((columns, high - low), jnp.bfloat16)],
        compiler_params=PARAMS,
        cost_estimate=pl.CostEstimate(
            flops=2 * rows * columns * (high - low),
            bytes_accessed=rows * columns * 4,
            transcendentals=0,
        ),
    )(w, *zs)


def own_kernel(me, x_ref, w_ref, *refs):
    firsts, rests = refs[:SPAN], refs[SPAN : 2 * SPAN]
    out_ref, z_cat = refs[2 * SPAN :]
    members, cut = x_ref.shape[1], rests[0].shape[1]

    @pl.when(pl.program_id(0) == 0)
    def _():
        fill(z_cat.at[:, :cut], rests, 0, cut)
        fill(z_cat.at[:, cut:], firsts, members, 2 * members - cut)

    out_ref[...] = x_ref[...] + jnp.dot(
        w_ref[...], z_cat[...], preferred_element_type=jnp.float32
    )


def own_terms(me, perturb, w, zs):
    share, columns = w.shape
    members = perturb.shape[1]
    tile = min(share, 128)
    steps = share // tile
    row = lambda n: pl.BlockSpec((tile, n), lambda i, *_: (i, 0))
    return pl.pallas_call(
        own_kernel,
        out_shape=jax.ShapeDtypeStruct((share, members), jnp.float32),
        grid_spec=pltpu.PrefetchScalarGridSpec(
            num_scalar_prefetch=1,
            grid=(steps,),
            in_specs=[
                pl.BlockSpec((tile, members), lambda i, me: (me[0] * steps + i, 0)),
                row(columns),
            ]
            + [WHOLE] * len(zs),
            out_specs=row(members),
            scratch_shapes=[pltpu.VMEM((columns, members), jnp.bfloat16)],
        ),
        compiler_params=PARAMS,
        cost_estimate=pl.CostEstimate(
            flops=2 * share * columns * members,
            bytes_accessed=share * members * 8,
            transcendentals=0,
        ),
        name="own",
    )(me, in_hbm(perturb), w, *zs)


def join_kernel(into, base_ref, *refs):
    pieces, out_ref = refs[:-1], refs[-1]
    if into:
        pieces = pieces[:-1]
    total = base_ref[...]
    for piece in pieces:
        total = total + piece[...].astype(jnp.float32)
    out_ref[...] = total


def join(base, pieces, low, high, into):
    share, members = base.shape
    part = high - low
    block = math.gcd(low, part)
    tile = min(share, 256)
    span = pl.BlockSpec((tile, block), lambda i, j: (i, low // block + j))
    piece = pl.BlockSpec((tile, block), lambda i, j: (i, j))
    extra = [] if into is None else [into]
    return pl.pallas_call(
        functools.partial(join_kernel, into is not None),
        out_shape=jax.ShapeDtypeStruct((share, members), jnp.float32),
        grid=(share // tile, part // block),
        in_specs=[span] + [piece] * len(pieces) + [pl.BlockSpec(memory_space=pl.ANY)] * len(extra),
        out_specs=span,
        input_output_aliases={1 + len(pieces): 0} if extra else {},
        compiler_params=PARAMS,
        cost_estimate=pl.CostEstimate(
            flops=share * part, bytes_accessed=share * part * 10, transcendentals=0
        ),
    )(base, *pieces, *extra)


def update(perturb, observed, solved, taper_index, taper_table):
    groups = lax.axis_size("obs")
    share = perturb.shape[0] // groups
    me = lax.axis_index("obs").astype(jnp.int32).reshape(1)
    slot = slots()
    members = perturb.shape[1]
    cut = member_cut(members)

    first, rest = pack(observed, solved, cut)
    first_near = swap(first)
    first_far = gather_far(first)
    rests = (rest, swap(rest)) + gather_far(rest)
    firsts = (first, first_near) + first_far
    xb, near, kept = near_terms(
        perturb, taper_index, taper_table, me, slot, first, first_near, share
    )
    w_sent = weigh(slot, taper_table, xb, kept, near, first_far)
    w_own = weigh_own(me, slot, taper_table, perturb, taper_index, firsts, share)

    def exchange(part):
        return [
            permute(part[(step - 1) * share : step * share], "obs", lambda s: s + step)
            for step in range(1, groups)
        ]

    came_first = exchange(part_terms(w_sent, firsts, members, 2 * members - cut))
    came_rest = exchange(part_terms(w_sent, rests, 0, cut))
    base = own_terms(me, perturb, w_own, firsts + rests)
    out = join(base, came_first, cut, members, None)
    return join(base, came_rest, 0, cut, out)


def solution(mesh):
    placed = (
        P("lon", None),
        P(("lon", "obs"), None),
        P(("lon", "obs"), None),
        P("lon", "obs"),
        P(),
    )
    return jax.shard_map(
        update, mesh=mesh, in_specs=placed, out_specs=P(("lon", "obs"), None), check_vma=False
    )
```
